256 devices in a mesh: blk: 32 (over z, x_lo, core), head: 8 (over x_hi, y).
Axes of the slice: x: 4 (x_hi: 2, x_lo: 2; x = x_hi * 2 + x_lo), y: 4, z: 8, core: 2. Of those that a mesh axis runs over, the one named last changes fastest.
Arguments:
- query_tokens: bfloat16 [16384, 3072], P(('blk', 'head')), may hold values from -12 to 12
- key_tokens: bfloat16 [16384, 3072], P(('blk', 'head')), may hold values from -6 to 6
- value_tokens: bfloat16 [16384, 3072], P(('blk', 'head')), may hold values from -6 to 6
- out_weight: bfloat16 [3072, 3072], P('head'), may hold values from -1.75 to 1.75
- kv_blocks: int32 [128, 16], P('blk'), may hold values from -1 to 127, as said below
Outputs:
- projected: bfloat16 [16384, 3072], P(('blk', 'head'))
The draws below stay inside these ranges and needn't reach their ends.
Inputs may be any that keep to these rules, and one draw needn't show every extreme that they name: `kv_blocks`: row i lists the key blocks of 128 tokens that query block i attends to; let G = floor(i / 4). Entry 0 is i. Entry 1 is one of the blocks 4 * M to 4 * M + 3 with M = (G + 16) mod 32. Entry j >= 2 is -1 (absent) or one of the blocks 4 * (G + o) to 4 * (G + o) + 3, with o = j // 2 for even j and o = -(j - 1) // 2 for odd j; it is present whenever j < 8 and those blocks exist. Entries of one row are distinct.
All inputs are finite; a program needn't handle non-finite values.
Results may differ from the reference program's by a relative error of at most 0.012.
Values may be sent and summed in bfloat16 or wider, within the bound.
A program may use at most 128 MiB of HBM per device.

```python
import math
import jax
import jax.numpy as jnp
from jax import lax

HEADS = 24
HD = 128
D = 3072
BLOCK = 128
NSEL = 16
SEQ = 16384
QBLOCKS = 128
QBD = 4
N_HEAD = 8


def draw_query_tokens(key, part):
    drawn = jax.random.truncated_normal(jax.random.fold_in(key, 1), -6.0, 6.0, (SEQ, D), jnp.float32)
    return drawn.astype(jnp.bfloat16)


def draw_key_tokens(key, part):
    drawn = jax.random.truncated_normal(jax.random.fold_in(key, 2), -6.0, 6.0, (SEQ, D), jnp.float32)
    return drawn.astype(jnp.bfloat16)


def draw_kv_blocks(key, part):
    block_ids = jnp.arange(QBLOCKS, dtype=jnp.int32)
    groups = QBLOCKS // QBD
    owner = block_ids // QBD
    slot_ids = jnp.arange(NSEL, dtype=jnp.int32)
    offsets = slot_ids // 2 * jnp.where(slot_ids % 2 == 0, 1, -1)
    near_target = owner[:, None] + offsets[None, :]
    mirror = ((owner + groups // 2) % groups)[:, None]
    target = jnp.where(slot_ids[None, :] == 1, mirror, near_target)
    inside = jax.random.randint(jax.random.fold_in(key, 21), (QBLOCKS, NSEL), 0, QBD)
    chosen_block = jnp.where(slot_ids[None, :] == 0, block_ids[:, None], target * QBD + inside)
    counts = jax.random.randint(jax.random.fold_in(key, 22), (QBLOCKS, 1), NSEL // 2, NSEL + 1)
    present = (target >= 0) & (target < groups) & (slot_ids[None, :] < counts)
    return jnp.where(present, chosen_block, -1).astype(jnp.int32)


def steps_of(rng, dims, shards, low, top_value):
    loudness, own = 1.0, jax.random.fold_in(rng, 6)
    for dim, parts in shards:
        heights = jnp.exp(jax.random.uniform(jax.random.fold_in(own, dim), (parts,), jnp.float32, low / len(shards), top_value / len(shards)))
        loudness = loudness * jnp.repeat(heights, dims[dim] // parts).reshape([-1 if axis == dim else 1 for axis in range(len(dims))])
    return loudness


def normal_values(rng, extent, width, reach, shards=(), kind=jnp.bfloat16):
    result = width * jax.random.normal(rng, extent, jnp.float32)
    if shards:
        result = result * steps_of(rng, extent, shards, -0.22, 0.18)
    return jnp.clip(result, -reach, reach).astype(kind)


def setup_inputs(seed: int = 0) -> dict:
    splits = jax.random.split(jax.random.key(seed), 6)
    query_tokens = draw_query_tokens(jax.random.fold_in(splits[5], 71), 0)
    key_tokens = draw_key_tokens(jax.random.fold_in(splits[5], 71), 0)
    value_tokens = normal_values(splits[2], (SEQ, D), 1.0, 6.0, ((0, 256),))
    out_weight = normal_values(splits[3], (D, D), (D // 256) ** -0.5, 1.75, ((0, 8),))
    kv_blocks = draw_kv_blocks(jax.random.fold_in(splits[5], 71), 0)
    return {"query_tokens": query_tokens, "key_tokens": key_tokens, "value_tokens": value_tokens, "out_weight": out_weight, "kv_blocks": kv_blocks}


masked_low = -1e+30

def reference(query_tokens, key_tokens, value_tokens, out_weight, kv_blocks):
    query_blocks = query_tokens.reshape(QBLOCKS, BLOCK, HEADS, HD)
    key_blocks = key_tokens.reshape(QBLOCKS, BLOCK, HEADS, HD)
    value_blocks = value_tokens.reshape(QBLOCKS, BLOCK, HEADS, HD)
    scaling = 1.0 / math.sqrt(HD)

    def one_block(block_index):
        listed = kv_blocks[block_index]
        present = listed >= 0
        safe_index = jnp.maximum(listed, 0).astype(jnp.int32)
        keys_here = key_blocks[safe_index].astype(jnp.float32)
        values_here = value_blocks[safe_index].astype(jnp.float32)
        queries_here = query_blocks[block_index].astype(jnp.float32)
        scores = jnp.einsum('qhd,nkhd->hqnk', queries_here, keys_here) * scaling
        allowed = present[None, None, :, None]
        peak_value = lax.optimization_barrier(jnp.max(jnp.where(allowed, scores, masked_low), axis=(2, 3), keepdims=True))
        weights = jnp.where(allowed, jnp.exp(scores - peak_value), 0.0)
        denom = lax.optimization_barrier(jnp.sum(weights, axis=(2, 3)))
        probs = lax.optimization_barrier(weights.astype(jnp.bfloat16)).astype(jnp.float32)
        outputs = jnp.einsum('hqnk,nkhd->hqd', probs, values_here) / denom[..., None]
        return jnp.transpose(outputs, (1, 0, 2)).reshape(BLOCK, D).astype(jnp.bfloat16)
    attended = lax.map(one_block, jnp.arange(QBLOCKS, dtype=jnp.int32)).reshape(SEQ, D)
    group_width = D // N_HEAD
    running_sum = jnp.zeros((SEQ, D), jnp.float32)
    for group in range(N_HEAD):
        partial_term = jnp.dot(attended[:, group * group_width:(group + 1) * group_width], out_weight[group * group_width:(group + 1) * group_width], preferred_element_type=jnp.float32).astype(jnp.bfloat16)
        running_sum = running_sum + lax.optimization_barrier(partial_term).astype(jnp.float32)
    return running_sum.astype(jnp.bfloat16)
```

```python
import functools
import math

import jax
import jax.numpy as jnp
from jax import lax
from jax.experimental import pallas as pl
from jax.experimental.pallas import tpu as pltpu
from jax.sharding import PartitionSpec as P

HD = 128
BLOCK = 128
VM = pltpu.VMEM
F32 = jnp.float32
BF16 = jnp.bfloat16


def greet(n):
    me = lax.axis_index("head")
    barrier = pltpu.get_barrier_semaphore()
    for k in range(1, n):
        pl.semaphore_signal(barrier, inc=1, device_id={"head": lax.rem(me + k, n)})
    pl.semaphore_wait(barrier, n - 1)
    return me


def spread_kernel(n, q_ref, k_ref, v_ref, qo_ref, kvo_ref, send_sem, recv_sem, own_sem):
    rows = q_ref.shape[0]
    width = q_ref.shape[1] // n
    me = greet(n)
    here = pl.ds(pl.multiple_of(me * rows, rows), rows)

    def pieces(dest):
        cols = pl.ds(pl.multiple_of(dest * width, width), width)
        return (
            (k_ref.at[:, cols], kvo_ref.at[here, pl.ds(0, width)]),
            (v_ref.at[:, cols], kvo_ref.at[here, pl.ds(width, width)]),
            (q_ref.at[:, cols], qo_ref.at[here, :]),
        )

    copies = []
    for k in range(1, n):
        dest = lax.rem(me + k, n)
        for a, (src, dst) in enumerate(pieces(dest)):
            c = pltpu.make_async_remote_copy(
                src, dst, send_sem.at[k - 1, a], recv_sem.at[k - 1, a], device_id={"head": dest}
            )
            c.start()
            copies.append(c)
    own = []
    for a, (src, dst) in enumerate(pieces(me)):
        c = pltpu.make_async_copy(src, dst, own_sem.at[a])
        c.start()
        own.append(c)
    for c in own:
        c.wait()
    for c in copies:
        c.wait()


def spread(n, q, k, v):
    rows, full = q.shape
    width = full // n
    whole = pl.BlockSpec(memory_space=VM)
    return pl.pallas_call(
        functools.partial(spread_kernel, n),
        out_shape=(
            jax.ShapeDtypeStruct((rows * n, width), BF16),
            jax.ShapeDtypeStruct((rows * n, 2 * width), BF16),
        ),
        in_specs=[whole] * 3,
        out_specs=(whole, whole),
        scratch_shapes=[
            pltpu.SemaphoreType.DMA((n - 1, 3)),
            pltpu.SemaphoreType.DMA((n - 1, 3)),
            pltpu.SemaphoreType.DMA((3,)),
        ],
        compiler_params=pltpu.CompilerParams(collective_id=0, has_side_effects=True),
    )(q, k, v)


def reduce_kernel(n, x_ref, o_ref, held, send_sem, recv_sem):
    rows = o_ref.shape[0]
    me = greet(n)
    copies = []
    for k in range(1, n):
        dest = lax.rem(me + k, n)
        c = pltpu.make_async_remote_copy(
            x_ref.at[pl.ds(pl.multiple_of(dest * rows, rows), rows), :],
            held.at[k - 1],
            send_sem.at[k - 1],
            recv_sem.at[k - 1],
            device_id={"head": dest},
        )
        c.start()
        copies.append(c)
    for c in copies:
        c.wait()
    mine = pl.ds(pl.multiple_of(me * rows, rows), rows)
    step = 512

    def add(i, carry):
        cols = pl.ds(pl.multiple_of(i * step, step), step)
        total = x_ref[mine, cols].astype(F32)
        for k in range(n - 1):
            total = total + held[k, :, cols].astype(F32)
        o_ref[:, cols] = total.astype(BF16)
        return carry

    lax.fori_loop(0, o_ref.shape[1] // step, add, 0)


def reduce_rows(n, x):
    rows = x.shape[0] // n
    whole = pl.BlockSpec(memory_space=VM)
    return pl.pallas_call(
        functools.partial(reduce_kernel, n),
        out_shape=jax.ShapeDtypeStruct((rows, x.shape[1]), BF16),
        in_specs=[whole],
        out_specs=whole,
        scratch_shapes=[
            VM((n - 1, rows, x.shape[1]), BF16),
            pltpu.SemaphoreType.DMA((n - 1,)),
            pltpu.SemaphoreType.DMA((n - 1,)),
        ],
        compiler_params=pltpu.CompilerParams(collective_id=1, has_side_effects=True),
    )(x)


def attend_kernel(slots, heads, index_ref, q_ref, bias_ref, *refs):
    ks, vs = refs[:slots], refs[slots : 2 * slots]
    w_ref, o_ref = refs[2 * slots], refs[2 * slots + 1]
    scaling = 1.0 / math.sqrt(HD)
    done = []
    for h in range(heads):
        cols = slice(h * HD, (h + 1) * HD)
        keys = jnp.concatenate([r[:, cols] for r in ks], axis=0)
        values = jnp.concatenate([r[:, cols] for r in vs], axis=0)
        scores = lax.dot_general(
            q_ref[:, cols], keys, (((1,), (1,)), ((), ())), preferred_element_type=F32
        )
        scores = scores * scaling + bias_ref[0]
        peak = jnp.max(scores, axis=-1, keepdims=True)
        weights = jnp.exp(scores - peak)
        denom = jnp.sum(weights, axis=-1, keepdims=True)
        out = jnp.dot(weights.astype(BF16), values, preferred_element_type=F32)
        done.append((out / denom).astype(BF16))
    attended = jnp.concatenate(done, axis=1)
    o_ref[...] = jnp.dot(attended, w_ref[...], preferred_element_type=F32).astype(BF16)


def attend(queries, kv, weight, kv_blocks):
    blocks, slots = kv_blocks.shape
    width = queries.shape[1]
    heads = width // HD
    bias = jnp.where(kv_blocks >= 0, 0.0, -1e30).astype(F32)
    bias = jnp.repeat(bias, BLOCK, axis=1).reshape(blocks, 1, slots * BLOCK)
    index = jnp.maximum(kv_blocks, 0)

    def side(j, half):
        return pl.BlockSpec((BLOCK, width), lambda i, idx: (idx[i, j], half))

    return pl.pallas_call(
        functools.partial(attend_kernel, slots, heads),
        out_shape=jax.ShapeDtypeStruct((queries.shape[0], weight.shape[1]), BF16),
        grid_spec=pltpu.PrefetchScalarGridSpec(
            num_scalar_prefetch=1,
            grid=(blocks,),
            in_specs=[
                pl.BlockSpec((BLOCK, width), lambda i, idx: (i, 0)),
                pl.BlockSpec((1, 1, slots * BLOCK), lambda i, idx: (i, 0, 0)),
            ]
            + [side(j, 0) for j in range(slots)]
            + [side(j, 1) for j in range(slots)]
            + [pl.BlockSpec(weight.shape, lambda i, idx: (0, 0))],
            out_specs=pl.BlockSpec((BLOCK, weight.shape[1]), lambda i, idx: (i, 0)),
        ),
        compiler_params=pltpu.CompilerParams(vmem_limit_bytes=48 << 20),
    )(index, queries, bias, *([kv] * (2 * slots)), weight)


def on_device(n, query_tokens, key_tokens, value_tokens, out_weight, kv_blocks):
    queries, kv = spread(n, query_tokens, key_tokens, value_tokens)
    gathered = lax.all_gather(kv, "blk", axis=0, tiled=True)
    partial = attend(queries, gathered, out_weight, kv_blocks)
    return reduce_rows(n, partial)


def solution(mesh):
    placed = (
        P(("blk", "head"), None),
        P(("blk", "head"), None),
        P(("blk", "head"), None),
        P("head", None),
        P("blk", None),
    )
    return jax.shard_map(
        functools.partial(on_device, mesh.shape["head"]),
        mesh=mesh,
        in_specs=placed,
        out_specs=P(("blk", "head"), None),
        check_vma=False,
    )
```
